32 devices in a mesh: rows: 8 (over z, y), batch: 4 (over x, core).
Axes of the slice: x: 2, y: 2, z: 4, core: 2. Of those that a mesh axis runs over, the one named last changes fastest.
Arguments:
- patches: bfloat16 [16, 56, 56, 384], P('batch', 'rows'), may hold values from -6 to 6
- widths: int32 [16], P('batch'), may hold values from 29 to 56, as said below
- keep_mask: int32 [16, 2], P('batch'), may hold values 0 or 1
- pre_gain: bfloat16 [384], replicated, may hold values from 0.5 to 1.5
- pre_shift: bfloat16 [384], replicated, may hold values from -3 to 3
- in_weight: bfloat16 [384, 1152], replicated, may hold values from -0.3125 to 0.3125
- in_bias: bfloat16 [768], replicated, may hold values from -3 to 3
- bias_table: bfloat16 [169, 12], replicated, may hold values from -4 to 4
- out_weight: bfloat16 [384, 384], replicated, may hold values from -1.25 to 1.25
- out_bias: bfloat16 [384], replicated, may hold values from -3 to 3
- mid_gain: bfloat16 [384], replicated, may hold values from 0.5 to 1.5
- mid_shift: bfloat16 [384], replicated, may hold values from -3 to 3
- up_weight: bfloat16 [384, 1536], replicated, may hold values from -0.3125 to 0.3125
- up_bias: bfloat16 [1536], replicated, may hold values from -3 to 3
- down_weight: bfloat16 [1536, 384], replicated, may hold values from -0.15625 to 0.15625
- down_bias: bfloat16 [384], replicated, may hold values from -3 to 3
- cotangent: bfloat16 [16, 56, 56, 384], P('batch', 'rows'), may hold values from -6 to 6
Outputs:
- output: bfloat16 [16, 56, 56, 384], P('batch', 'rows')
- grad_patches: float32 [16, 56, 56, 384], P('batch', 'rows')
- grad_pre_gain: float32 [384], replicated
- grad_pre_shift: float32 [384], replicated
- grad_in_weight: float32 [384, 1152], replicated
- grad_in_bias: float32 [768], replicated
- grad_bias_table: float32 [169, 12], replicated
- grad_out_weight: float32 [384, 384], replicated
- grad_out_bias: float32 [384], replicated
- grad_mid_gain: float32 [384], replicated
- grad_mid_shift: float32 [384], replicated
- grad_up_weight: float32 [384, 1536], replicated
- grad_up_bias: float32 [1536], replicated
- grad_down_weight: float32 [1536, 384], replicated
- grad_down_bias: float32 [384], replicated
The draws below stay inside these ranges and needn't reach their ends.
Inputs may be any that keep to these rules, and one draw needn't show every extreme that they name: `widths`: every draw holds an image of the full canvas width 56 and one of width 56 // 2 + 1.
All inputs are finite; a program needn't handle non-finite values. No bound on the sum of `keep_mask` on one device may be relied on, other than what follows from the above.
Results may differ from the reference program's by a relative error of at most 0.012.
Values may be sent and summed in bfloat16 or wider, within the bound.
No kernel may reach another device: no remote copies, remote signals or barrier semaphores. Data moves between devices by JAX's collectives and lax.ppermute only.
A program may use at most 192 MiB of HBM per device.

```python
import math
import jax
import jax.numpy as jnp
from jax import lax

C = 384
HEADS = 12
FF = 1536
WIN = 7
SHIFT = 3
TABLE = 169
WIDTH = 56
HEIGHT = 56
IMAGES = 16


def draw_widths(key, part):
    key_one, key_two = jax.random.split(jax.random.fold_in(key, 17))
    drawn = jax.random.randint(key_one, (IMAGES,), WIDTH // 2 + 1, WIDTH + 1)
    chosen = jax.random.randint(key_two, (), 0, IMAGES)
    places = jnp.arange(IMAGES)
    drawn = jnp.where(places == chosen, WIDTH, drawn)
    drawn = jnp.where(places == (chosen + 1) % IMAGES, WIDTH // 2 + 1, drawn)
    return drawn.astype(jnp.int32)


def set_ends(values, rng, smallest, top_value):
    longest = values.shape.index(max(values.shape))
    spots = []
    for shift in (0, 1):
        where = [jax.random.randint(jax.random.fold_in(rng, axis), (), 0, length) for axis, length in enumerate(values.shape)]
        where[longest] = (where[longest] + shift) % values.shape[longest]
        spots.append(tuple(where))
    return values.at[spots[0]].set(smallest).at[spots[1]].set(top_value)


def block_scale(own_key, extent, pieces, low, high):
    def one(position, parts):
        steps = jax.random.uniform(jax.random.fold_in(jax.random.fold_in(own_key, 6), position), (parts,), jnp.float32, low / len(pieces), high / len(pieces))
        return jnp.repeat(jnp.exp(steps), extent[position] // parts).reshape((-1,) + (1,) * (len(extent) - position - 1))

    level = one(*pieces[0])
    for cut in pieces[1:]:
        level = level * one(*cut)
    return level


def scatter_about(key, dims, scale, limit, shards=(), kind=jnp.bfloat16):
    values = scale * jax.random.normal(key, dims, jnp.float32)
    if shards:
        values = values * block_scale(key, dims, shards, -0.22, 0.18)
    return jnp.clip(values, -limit, limit).astype(kind)


def setup_inputs(seed: int = 0) -> dict:
    arg_keys = jax.random.split(jax.random.key(seed), 18)
    return {
        "patches": scatter_about(arg_keys[0], (IMAGES, HEIGHT, WIDTH, C), 1.0, 6.0, ((0, 4), (1, 8))),
        "widths": draw_widths(jax.random.fold_in(arg_keys[17], 71), 0),
        "keep_mask": set_ends((jax.random.randint(arg_keys[2], (IMAGES, 2), 0, 5) < 4).astype(jnp.int32), jax.random.fold_in(arg_keys[2], 1), 0, 1),
        "pre_gain": jnp.clip(1.0 + 0.1 * jax.random.normal(arg_keys[3], (C,), jnp.float32), 0.5, 1.5).astype(jnp.bfloat16),
        "pre_shift": scatter_about(arg_keys[4], (C,), 0.5, 3.0),
        "in_weight": scatter_about(arg_keys[5], (C, 3 * C), C ** -0.5, 0.3125),
        "in_bias": scatter_about(arg_keys[6], (2 * C,), 0.5, 3.0),
        "bias_table": scatter_about(arg_keys[7], (TABLE, HEADS), 1.0, 4.0),
        "out_weight": scatter_about(arg_keys[8], (C, C), (C // 16) ** -0.5, 1.25),
        "out_bias": scatter_about(arg_keys[9], (C,), 0.5, 3.0),
        "mid_gain": jnp.clip(1.0 + 0.1 * jax.random.normal(arg_keys[10], (C,), jnp.float32), 0.5, 1.5).astype(jnp.bfloat16),
        "mid_shift": scatter_about(arg_keys[11], (C,), 0.5, 3.0),
        "up_weight": scatter_about(arg_keys[12], (C, FF), C ** -0.5, 0.3125),
        "up_bias": scatter_about(arg_keys[13], (FF,), 0.5, 3.0),
        "down_weight": scatter_about(arg_keys[14], (FF, C), FF ** -0.5, 0.15625),
        "down_bias": scatter_about(arg_keys[15], (C,), 0.5, 3.0),
        "cotangent": scatter_about(arg_keys[16], (IMAGES, HEIGHT, WIDTH, C), 1.0, 6.0, ((0, 4), (1, 8))),
    }


HIGHEST = lax.Precision.HIGHEST
EPSILON = 1e-05
KEEP_RATE = 0.8
MASKED = -100.0

@jax.custom_vjp
def low(v):
    return lax.optimization_barrier(v.astype(jnp.bfloat16)).astype(jnp.float32)

@jax.custom_vjp
def low_back(v):
    return v

def low_keep(v):
    return (low(v), None)

def low_pass(kept, grad):
    return (grad,)

def back_keep(v):
    return (v, None)

def back_low(kept, grad):
    return (low(grad),)
low.defvjp(low_keep, low_pass)
low_back.defvjp(back_keep, back_low)

def rounded_both(values):
    return low(low_back(values))

def layer_norm(values, gain, shift):
    centred = values - lax.optimization_barrier(jnp.mean(values, axis=-1, keepdims=True))
    spread = lax.optimization_barrier(jnp.mean(centred * centred, axis=-1, keepdims=True))
    return centred * lax.rsqrt(spread + EPSILON) * gain + shift

def to_windows(canvas):
    images, height, columns, channels = canvas.shape
    blocked = canvas.reshape(images, height // WIN, WIN, columns // WIN, WIN, channels)
    return blocked.transpose(0, 1, 3, 2, 4, 5).reshape(-1, WIN * WIN, channels)

def from_windows(blocked, images, height, columns):
    channels = blocked.shape[-1]
    canvas = blocked.reshape(images, height // WIN, columns // WIN, WIN, WIN, channels)
    return canvas.transpose(0, 1, 3, 2, 4, 5).reshape(images, height, columns, channels)

def table_onehot():
    places = jnp.arange(WIN * WIN, dtype=jnp.int32)
    row_pos = places // WIN
    col_pos = places % WIN
    table_index = (row_pos[:, None] - row_pos[None, :] + WIN - 1) * (2 * WIN - 1) + (col_pos[:, None] - col_pos[None, :] + WIN - 1)
    entries = jnp.arange((2 * WIN - 1) ** 2, dtype=jnp.int32)
    return table_index.reshape(-1)[:, None] == entries[None, :]

def region_ids(row_glob, total_rows, columns):
    row_region = (row_glob >= total_rows - WIN).astype(jnp.int32) + (row_glob >= total_rows - SHIFT).astype(jnp.int32)
    col_glob = jnp.arange(columns, dtype=jnp.int32)
    col_region = (col_glob >= columns - WIN).astype(jnp.int32) + (col_glob >= columns - SHIFT).astype(jnp.int32)
    return row_region[:, None] * 3 + col_region[None, :]

def image_block(weights, patch_img, width_img, keep_img):
    pre_gain, pre_shift, in_weight, in_bias, bias_table, out_weight, out_bias, mid_gain, mid_shift, up_weight, up_bias, down_weight, down_bias = weights
    head_size = C // HEADS
    factor = 1.0 / math.sqrt(head_size)
    shifted = jnp.roll(patch_img, (-SHIFT, -SHIFT), axis=(0, 1))
    tokens = to_windows(shifted[None]).reshape(-1, C)
    window_count = tokens.shape[0] // (WIN * WIN)
    col_glob = jnp.arange(WIDTH, dtype=jnp.int32)
    valid_cols = ((col_glob + SHIFT) % WIDTH < width_img).astype(jnp.float32)
    valid_grid = jnp.broadcast_to(valid_cols[None, None, :, None], (1, HEIGHT, WIDTH, 1))
    valid_tok = to_windows(valid_grid).reshape(-1, 1)
    keep_rates = keep_img.astype(jnp.float32) / KEEP_RATE
    regions = region_ids(jnp.arange(HEIGHT, dtype=jnp.int32), HEIGHT, WIDTH)
    region_win = to_windows(jnp.broadcast_to(regions[None, :, :, None], (1, HEIGHT, WIDTH, 1)))[:, :, 0]
    shift_add = jnp.where(region_win[:, :, None] == region_win[:, None, :], 0.0, MASKED).astype(jnp.float32)
    pair_bias = jnp.dot(table_onehot().astype(jnp.float32), bias_table, precision=HIGHEST, preferred_element_type=jnp.float32)
    pair_bias = pair_bias.T.reshape(HEADS, WIN * WIN, WIN * WIN)
    hidden_one = low(layer_norm(tokens, pre_gain, pre_shift) * valid_tok)
    bias_full = jnp.concatenate([in_bias[:C], jnp.zeros((C,), jnp.float32), in_bias[C:]])
    projected = jnp.dot(hidden_one, in_weight, precision=HIGHEST, preferred_element_type=jnp.float32) + bias_full
    heads_shape = (window_count, WIN * WIN, HEADS, head_size)
    queries = rounded_both(projected[:, :C]).reshape(heads_shape)
    keys_all = rounded_both(projected[:, C:2 * C]).reshape(heads_shape)
    vals_all = rounded_both(projected[:, 2 * C:]).reshape(heads_shape)
    scores = jnp.einsum('wqhd,wkhd->whqk', queries, keys_all, precision=HIGHEST) * factor
    scores = low_back(scores + pair_bias[None] + shift_add[:, None])
    probs = low(jax.nn.softmax(scores, axis=-1))
    mixed = jnp.einsum('whqk,wkhd->wqhd', probs, vals_all, precision=HIGHEST).reshape(-1, C)
    mixed = rounded_both(mixed)
    attn_out = low_back(jnp.dot(mixed, out_weight, precision=HIGHEST, preferred_element_type=jnp.float32) + out_bias)
    after_attn = tokens + valid_tok * keep_rates[0] * attn_out
    hidden_two = low(layer_norm(after_attn, mid_gain, mid_shift))
    pre_act = low_back(jnp.dot(hidden_two, up_weight, precision=HIGHEST, preferred_element_type=jnp.float32) + up_bias)
    act_low = low(jax.nn.gelu(pre_act, approximate=False))
    mlp_out = low_back(jnp.dot(act_low, down_weight, precision=HIGHEST, preferred_element_type=jnp.float32) + down_bias)
    result = after_attn + valid_tok * keep_rates[1] * mlp_out
    return from_windows(result.reshape(window_count, WIN * WIN, C), 1, HEIGHT, WIDTH)[0]

def reference(patches, widths, keep_mask, pre_gain, pre_shift, in_weight, in_bias, bias_table, out_weight, out_bias, mid_gain, mid_shift, up_weight, up_bias, down_weight, down_bias, cotangent):
    params = tuple((weight.astype(jnp.float32) for weight in (pre_gain, pre_shift, in_weight, in_bias, bias_table, out_weight, out_bias, mid_gain, mid_shift, up_weight, up_bias, down_weight, down_bias)))

    def forward(inputs, *weights):

        def one_image(item):
            return image_block(weights, item[0], item[1], item[2])
        return lax.map(jax.checkpoint(one_image), (inputs, widths, keep_mask))
    result, pullback = jax.vjp(forward, patches.astype(jnp.float32), *params)
    grads = pullback(cotangent.astype(jnp.float32))
    return (result.astype(jnp.bfloat16), grads[0], grads[1], grads[2], grads[3], grads[4], grads[5], grads[6], grads[7], grads[8], grads[9], grads[10], grads[11], grads[12], grads[13])
```

```python
import math

import jax
import jax.numpy as jnp
from jax import lax
from jax.experimental import pallas as pl
from jax.experimental.pallas import tpu as pltpu
from jax.sharding import PartitionSpec as P

HEADS = 12
WIN = 7
SHIFT = 3
TOK = WIN * WIN
PAD = 56
GROUP = 4

EPSILON = 1e-05
KEEP_RATE = 0.8
MASKED = -100.0
EMPTY = -1e30

F32 = jnp.float32
BF16 = jnp.bfloat16


def nn(a, b):
    return lax.dot_general(a, b, (((1,), (0,)), ((), ())), preferred_element_type=F32)


def nt(a, b):
    return lax.dot_general(a, b, (((1,), (1,)), ((), ())), preferred_element_type=F32)


def tn(a, b):
    return lax.dot_general(a, b, (((0,), (0,)), ((), ())), preferred_element_type=F32)


def col_sum(a):
    return jnp.sum(a, axis=0, keepdims=True)


def row_mean(a):
    return jnp.mean(a, axis=-1, keepdims=True)


def normed(v):
    centred = v - row_mean(v)
    root = lax.rsqrt(row_mean(centred * centred) + EPSILON)
    return centred * root, root


def head_masks():
    lane = lax.broadcasted_iota(jnp.int32, (PAD, 128), 1)
    return [(lane >= 32 * h) & (lane < 32 * (h + 1)) for h in range(GROUP)]


def stacked(pair, masks):
    a, b = pair[:PAD], pair[PAD:]
    rows = [
        jnp.concatenate([jnp.where(m, a, 0.0), jnp.where(m, b, 0.0)], axis=1) for m in masks
    ]
    return jnp.concatenate(rows, axis=0).astype(BF16)


def diagonal(pair):
    a, b = pair[:PAD], pair[PAD:]
    z = jnp.zeros_like(a)
    return jnp.concatenate(
        [jnp.concatenate([a, z], axis=1), jnp.concatenate([z, b], axis=1)], axis=0
    ).astype(BF16)


def undiagonal(m):
    return jnp.concatenate([m[:PAD, :128], m[PAD:, 128:]], axis=0)


def unstacked(m, masks):
    sides = []
    for side in range(2):
        total = None
        for h, mask in enumerate(masks):
            piece = jnp.where(mask, m[h * PAD : (h + 1) * PAD, side * 128 : (side + 1) * 128], 0.0)
            total = piece if total is None else total + piece
        sides.append(total)
    return jnp.concatenate(sides, axis=0)


def normal_cdf_pdf(v):
    e = jnp.exp(-0.5 * (v * v))
    t = 1.0 / (1.0 + (0.3275911 / math.sqrt(2.0)) * jnp.abs(v))
    poly = 1.061405429
    for c in (-1.453152027, 1.421413741, -0.284496736, 0.254829592):
        poly = poly * t + c
    half_tail = (0.5 * poly) * t * e
    cdf = jnp.where(v >= 0.0, 1.0 - half_tail, half_tail)
    return cdf, e * (1.0 / math.sqrt(2.0 * math.pi))


def forward_kernel(
    widths_ref,
    keep_ref,
    own_ref,
    halo_ref,
    cot_ref,
    p_own_ref,
    p_halo_ref,
    p_cot_ref,
    p_out_ref,
    col_ref,
    bias_ref,
    vec_ref,
    up_bias_ref,
    in_w_ref,
    out_w_ref,
    up_w_ref,
    down_w_ref,
    out_ref,
    xs_ref,
    qkv_ref,
    prob_ref,
    grad_after_ref,
    grad_mixed_ref,
    acc_ref,
    proj_sc,
    mixed_sc,
    down_sc,
):
    i = pl.program_id(0)
    last = pl.num_programs(0) - 1
    channels = own_ref.shape[-1]
    hidden = up_w_ref.shape[1]
    chunks = hidden // channels
    groups = channels // 128
    pairs = proj_sc.shape[0] // (2 * PAD)
    factor = 1.0 / math.sqrt(channels // HEADS)

    @pl.when(i == 0)
    def _():
        acc_ref[...] = jnp.zeros_like(acc_ref)
        down_sc[...] = jnp.zeros_like(down_sc)

    def vec(n):
        return vec_ref[n : n + 1, :]

    valid = (col_ref[...] < widths_ref[i]).astype(F32)
    ka = keep_ref[i, 0].astype(F32) / KEEP_RATE
    kb = keep_ref[i, 1].astype(F32) / KEEP_RATE
    valid_a = valid * ka
    valid_b = valid * kb

    xs = nn(p_own_ref[...], own_ref[0]) + nn(p_halo_ref[...], halo_ref[0])
    xs_ref[0] = xs.astype(BF16)
    norm_one, _ = normed(xs)
    hidden_one = ((norm_one * vec(0) + vec(1)) * valid).astype(BF16)
    for part in range(3):
        cols = slice(part * channels, (part + 1) * channels)
        projected = nn(hidden_one, in_w_ref[:, cols]) + vec(2 + part)
        proj_sc[:, cols] = projected
        qkv_ref[0, :, cols] = projected.astype(BF16)

    masks = head_masks()

    def one_pair(j, carry):
        rows = pl.ds(pl.multiple_of(j * 2 * PAD, 2 * PAD), 2 * PAD)
        edge = (j == pairs - 1).astype(jnp.int32)
        for g in range(groups):
            lanes = [
                slice(part * channels + g * 128, part * channels + (g + 1) * 128)
                for part in range(3)
            ]
            q = stacked(proj_sc[rows, lanes[0]], masks)
            k = diagonal(proj_sc[rows, lanes[1]])
            v = diagonal(proj_sc[rows, lanes[2]])
            scores = nt(k, q) * factor + bias_ref[edge, g]
            probs = []
            for side in (scores[:PAD], scores[PAD:]):
                e = jnp.exp(side - jnp.max(side, axis=0, keepdims=True))
                probs.append(e * (1.0 / col_sum(e)))
            probs = jnp.concatenate(probs, axis=0).astype(BF16)
            prob_ref[0, j, g] = probs
            mixed_sc[rows, lanes[0]] = unstacked(tn(probs, v), masks)
        return carry

    lax.fori_loop(0, pairs, one_pair, 0)

    mixed = mixed_sc[...].astype(BF16)
    after = xs + valid_a * (nn(mixed, out_w_ref[...]) + vec(5))
    norm_two, root_two = normed(after)
    hidden_two = (norm_two * vec(6) + vec(7)).astype(BF16)
    cot = nn(p_cot_ref[...], cot_ref[0])
    grad_mlp_wide = (cot * valid_b).astype(BF16)
    mlp = jnp.zeros_like(after)
    grad_hidden = jnp.zeros_like(after)
    up_base = hidden
    small = 2 * hidden + channels
    for c in range(chunks):
        cols = slice(c * channels, (c + 1) * channels)
        pre = nn(hidden_two, up_w_ref[:, cols]) + up_bias_ref[:, cols]
        cdf, pdf = normal_cdf_pdf(pre)
        act = (pre * cdf).astype(BF16)
        mlp = mlp + nn(act, down_w_ref[cols, :])
        grad_act = nt(grad_mlp_wide, down_w_ref[cols, :])
        grad_pre = (grad_act * (cdf + pre * pdf)).astype(BF16)
        grad_hidden = grad_hidden + nt(grad_pre, up_w_ref[:, cols])
        up_rows = slice(up_base + c * channels, up_base + (c + 1) * channels)
        acc_ref[up_rows, :] += tn(hidden_two, grad_pre)
        down_sc[:, cols] += tn(grad_mlp_wide, act)
        acc_ref[small + 4 + c : small + 5 + c, :] += col_sum(grad_pre.astype(F32))
    result = (after + valid_b * (mlp + vec(8))).astype(BF16)
    out_ref[0] = nn(p_out_ref[...], result).astype(BF16)

    d = grad_hidden * vec(6)
    grad_after = cot + root_two * (d - row_mean(d) - norm_two * row_mean(d * norm_two))
    grad_after_ref[0] = grad_after
    grad_attn = (grad_after * valid_a).astype(BF16)
    grad_mixed_ref[0] = nt(grad_attn, out_w_ref[...]).astype(BF16)
    acc_ref[2 * hidden : 2 * hidden + channels, :] += tn(mixed, grad_attn)
    acc_ref[small : small + 1, :] += col_sum(grad_hidden * norm_two)
    acc_ref[small + 1 : small + 2, :] += col_sum(grad_hidden)
    acc_ref[small + 2 : small + 3, :] += col_sum(grad_attn.astype(F32))
    acc_ref[small + 3 : small + 4, :] += col_sum(grad_mlp_wide.astype(F32))

    @pl.when(i == last)
    def _():
        for c in range(chunks):
            cols = slice(c * channels, (c + 1) * channels)
            acc_ref[cols, :] = down_sc[:, cols].T


def backward_kernel(
    widths_ref,
    xs_ref,
    qkv_ref,
    prob_ref,
    grad_after_ref,
    grad_mixed_ref,
    p_own_t_ref,
    p_halo_t_ref,
    col_ref,
    vec_ref,
    in_w_ref,
    grad_own_ref,
    grad_halo_ref,
    acc_ref,
    table_ref,
    proj_sc,
):
    i = pl.program_id(0)
    channels = xs_ref.shape[-1]
    groups = channels // 128
    pairs = proj_sc.shape[0] // (2 * PAD)
    factor = 1.0 / math.sqrt(channels // HEADS)

    @pl.when(i == 0)
    def _():
        acc_ref[...] = jnp.zeros_like(acc_ref)
        table_ref[...] = jnp.zeros_like(table_ref)

    def vec(n):
        return vec_ref[n : n + 1, :]

    valid = (col_ref[...] < widths_ref[i]).astype(F32)
    masks = head_masks()

    def one_pair(j, carry):
        rows = pl.ds(pl.multiple_of(j * 2 * PAD, 2 * PAD), 2 * PAD)
        for g in range(groups):
            lanes = [
                slice(part * channels + g * 128, part * channels + (g + 1) * 128)
                for part in range(3)
            ]
            pair_q = qkv_ref[0, rows, lanes[0]].astype(F32)
            pair_k = qkv_ref[0, rows, lanes[1]].astype(F32)
            pair_v = qkv_ref[0, rows, lanes[2]].astype(F32)
            pair_m = grad_mixed_ref[0, rows, lanes[0]].astype(F32)
            q = stacked(pair_q, masks)
            gm = stacked(pair_m, masks)
            k = diagonal(pair_k)
            v = diagonal(pair_v)
            probs_low = prob_ref[0, j, g]
            probs = probs_low.astype(F32)
            grad_v = undiagonal(nn(probs_low, gm))
            weighted = probs * nt(v, gm)
            scores = []
            for lo in (0, PAD):
                side = weighted[lo : lo + PAD]
                scores.append(side - probs[lo : lo + PAD] * col_sum(side))
            table_ref[g] += scores[0] + scores[1]
            grad_s = jnp.concatenate(scores, axis=0).astype(BF16)
            grad_k = undiagonal(nn(grad_s, q)) * factor
            grad_q = unstacked(tn(grad_s, k), masks) * factor
            proj_sc[rows, lanes[0]] = grad_q.astype(BF16)
            proj_sc[rows, lanes[1]] = grad_k.astype(BF16)
            proj_sc[rows, lanes[2]] = grad_v.astype(BF16)
        return carry

    lax.fori_loop(0, pairs, one_pair, 0)

    norm_one, root_one = normed(xs_ref[0].astype(F32))
    hidden_one = ((norm_one * vec(0) + vec(1)) * valid).astype(BF16)
    grad_hidden = jnp.zeros_like(norm_one)
    small = 3 * channels
    for part in range(3):
        cols = slice(part * channels, (part + 1) * channels)
        grad_proj = proj_sc[:, cols]
        acc_ref[cols, :] += tn(hidden_one, grad_proj)
        grad_hidden = grad_hidden + nt(grad_proj, in_w_ref[:, cols])
        if part != 1:
            row = small + 2 + part // 2
            acc_ref[row : row + 1, :] += col_sum(grad_proj.astype(F32))
    grad_hidden = grad_hidden * valid
    acc_ref[small : small + 1, :] += col_sum(grad_hidden * norm_one)
    acc_ref[small + 1 : small + 2, :] += col_sum(grad_hidden)
    d = grad_hidden * vec(0)
    grad_xs = grad_after_ref[0] + root_one * (
        d - row_mean(d) - norm_one * row_mean(d * norm_one)
    )
    high = grad_xs.astype(BF16)
    rest = (grad_xs - high.astype(F32)).astype(BF16)
    p_own_t = p_own_t_ref[...]
    grad_own_ref[0] = nn(p_own_t, high) + nn(p_own_t, rest)
    grad_halo_ref[0] = nn(p_halo_t_ref[...], high).astype(BF16)


def placements(height, columns):
    row = jnp.arange(columns // WIN * PAD, dtype=jnp.int32)
    place = row % PAD
    real = place < TOK
    s = jnp.where(real, place // WIN, 1000)
    t = row // PAD * WIN + place % WIN
    shifted = (t + SHIFT) % columns
    own = jnp.where(s < height - SHIFT, (s + SHIFT) * columns + shifted, -1)
    halo = jnp.where((s >= height - SHIFT) & real, (s - height + SHIFT) * columns + shifted, -1)
    plain = jnp.where(real, s * columns + t, -1)

    def hot(index, count, first=0):
        return index[:, None] == first + jnp.arange(count, dtype=jnp.int32)[None, :]

    def hot_t(index, count, first=0):
        return index[None, :] == first + jnp.arange(count, dtype=jnp.int32)[:, None]

    area = height * columns
    edge = SHIFT * columns
    mats = dict(
        own=hot(own, area),
        halo=hot(halo, edge),
        cot=hot(plain, area),
        out=hot_t(plain, area),
        own_t=hot_t(own, area - edge, edge),
        halo_t=hot_t(halo, edge),
    )
    col = jnp.where(real, shifted, 1 << 20)
    return {k: v.astype(BF16) for k, v in mats.items()}, col[:, None]


def pair_offsets():
    a = jnp.arange(TOK, dtype=jnp.int32)
    r, c = a // WIN, a % WIN
    span = 2 * WIN - 1
    index = (r[None, :] - r[:, None] + WIN - 1) * span + c[None, :] - c[:, None] + WIN - 1
    return index[None] == jnp.arange(span * span, dtype=jnp.int32)[:, None, None]


def score_bias(bias_table, last_row):
    hot = pair_offsets().astype(BF16).reshape(-1, TOK * TOK)
    bias = lax.dot_general(
        bias_table, hot, (((0,), (0,)), ((), ())), preferred_element_type=F32
    ).reshape(HEADS, TOK, TOK)
    a = jnp.arange(TOK, dtype=jnp.int32)
    cut = WIN - SHIFT
    row_region = (a // WIN >= cut) & last_row
    col_region = a % WIN >= cut
    row_same = row_region[:, None] == row_region[None, :]
    col_same = col_region[:, None] == col_region[None, :]
    inner = jnp.where(row_same, 0.0, MASKED).astype(F32)
    edge = jnp.where(row_same & col_same, 0.0, MASKED).astype(F32)

    def laid(mask):
        full = jnp.pad(
            bias + mask[None], ((0, 0), (0, 0), (0, PAD - TOK)), constant_values=0.0
        )
        full = jnp.pad(full, ((0, 0), (0, PAD - TOK), (0, 0)), constant_values=EMPTY)
        full = full.reshape(HEADS // GROUP, GROUP, PAD, PAD).transpose(0, 2, 1, 3)
        return full.reshape(HEADS // GROUP, PAD, GROUP * PAD)

    plain, right = laid(inner), laid(edge)
    return jnp.stack(
        [jnp.concatenate([plain, plain], axis=1), jnp.concatenate([plain, right], axis=1)]
    )


def whole(shape):
    return pl.BlockSpec(shape, lambda i: (0,) * len(shape), pipeline_mode=pl.Buffered(1))


def kept(shape):
    return pl.BlockSpec(shape, lambda i: (0,) * len(shape))


def by_image(shape):
    return pl.BlockSpec((1,) + shape, lambda i: (i,) + (0,) * len(shape))


def in_smem():
    return pl.BlockSpec(memory_space=pltpu.SMEM)


def power_bits(count):
    bits = count.bit_length() - 1
    assert 1 << bits == count
    return bits


def stage_orders(sizes):
    first = [("batch", 0)]
    rows = [("rows", b) for b in range(power_bits(sizes["rows"]))]
    batch = [("batch", b) for b in range(1, power_bits(sizes["batch"]))]
    lead = batch[:1] + rows[:2]
    rest = rows[2:] + batch[1:]
    orders = [lead[k:] + lead[:k] + rest for k in range(len(lead))]
    return first, orders


def swapped(value, axis, bit):
    count = lax.axis_size(axis)
    return lax.ppermute(value, axis, [(n, n ^ (1 << bit)) for n in range(count)])


def my_bit(axis, bit):
    return (lax.axis_index(axis) >> bit) & 1


def halved(value, stage):
    half = value.shape[0] // 2
    bit = my_bit(*stage)
    sent = lax.dynamic_slice_in_dim(value, (1 - bit) * half, half).astype(BF16)
    keep = lax.dynamic_slice_in_dim(value, bit * half, half)
    return keep + swapped(sent, *stage).astype(F32)


def doubled(value, stage):
    other = swapped(value, *stage)
    bit = my_bit(*stage)
    return jnp.where(
        bit == 0, jnp.concatenate([value, other]), jnp.concatenate([other, value])
    )


def summed_over_devices(value, cuts, sizes):
    first, orders = stage_orders(sizes)
    parts, start = [], 0
    for rows in cuts:
        parts.append(value[start : start + rows])
        start += rows
    for stage in first:
        parts = [halved(p, stage) for p in parts]
    for step in range(len(orders[0])):
        parts = [halved(p, orders[n % len(orders)][step]) for n, p in enumerate(parts)]
    parts = [p.astype(BF16) for p in parts]
    for step in reversed(range(len(orders[0]))):
        parts = [doubled(p, orders[n % len(orders)][step]) for n, p in enumerate(parts)]
    for stage in first:
        parts = [doubled(p, stage) for p in parts]
    return parts


def on_device(sizes, interpret, *args):
    (
        patches,
        widths,
        keep_mask,
        pre_gain,
        pre_shift,
        in_weight,
        in_bias,
        bias_table,
        out_weight,
        out_bias,
        mid_gain,
        mid_shift,
        up_weight,
        up_bias,
        down_weight,
        down_bias,
        cotangent,
    ) = args
    images, height, columns, channels = patches.shape
    hidden = up_weight.shape[1]
    area = height * columns
    edge = SHIFT * columns
    count = lax.axis_size("rows")
    padded = columns // WIN * PAD
    pairs = columns // WIN // 2
    groups = channels // 128
    chunks = hidden // channels

    halo = lax.ppermute(
        patches[:, :SHIFT].reshape(images, edge, channels),
        "rows",
        [(n, (n - 1) % count) for n in range(count)],
    )
    own = patches.reshape(images, area, channels)
    cot = cotangent.reshape(images, area, channels)
    mats, col = placements(height, columns)
    bias = score_bias(bias_table, lax.axis_index("rows") == count - 1)
    zero = jnp.zeros((channels,), F32)
    vecs = jnp.stack(
        [
            pre_gain.astype(F32),
            pre_shift.astype(F32),
            in_bias[:channels].astype(F32),
            zero,
            in_bias[channels:].astype(F32),
            out_bias.astype(F32),
            mid_gain.astype(F32),
            mid_shift.astype(F32),
            down_bias.astype(F32),
        ]
        + [zero] * 7
    )
    grid = (images,)
    params = pltpu.CompilerParams(
        dimension_semantics=("arbitrary",), vmem_limit_bytes=60 * 1024 * 1024
    )
    rows_one = 2 * hidden + channels + 128
    rows_two = 3 * channels + 128
    output, xs, qkv, probs, grad_after, grad_mixed, acc_one = pl.pallas_call(
        forward_kernel,
        grid=grid,
        in_specs=[
            in_smem(),
            in_smem(),
            by_image((area, channels)),
            by_image((edge, channels)),
            by_image((area, channels)),
            whole((padded, area)),
            whole((padded, edge)),
            whole((padded, area)),
            whole((area, padded)),
            whole((padded, 1)),
            whole(bias.shape),
            whole((16, channels)),
            whole((1, hidden)),
            whole((channels, 3 * channels)),
            whole((channels, channels)),
            whole((channels, hidden)),
            whole((hidden, channels)),
        ],
        out_specs=[
            by_image((area, channels)),
            by_image((padded, channels)),
            by_image((padded, 3 * channels)),
            by_image((pairs, groups, 2 * PAD, GROUP * PAD)),
            by_image((padded, channels)),
            by_image((padded, channels)),
            kept((rows_one, channels)),
        ],
        out_shape=[
            jax.ShapeDtypeStruct((images, area, channels), BF16),
            jax.ShapeDtypeStruct((images, padded, channels), BF16),
            jax.ShapeDtypeStruct((images, padded, 3 * channels), BF16),
            jax.ShapeDtypeStruct((images, pairs, groups, 2 * PAD, GROUP * PAD), BF16),
            jax.ShapeDtypeStruct((images, padded, channels), F32),
            jax.ShapeDtypeStruct((images, padded, channels), BF16),
            jax.ShapeDtypeStruct((rows_one, channels), F32),
        ],
        scratch_shapes=[
            pltpu.VMEM((padded, 3 * channels), F32),
            pltpu.VMEM((padded, channels), F32),
            pltpu.VMEM((channels, hidden), F32),
        ],
        compiler_params=params,
        interpret=interpret,
        name="forward_mlp",
    )(
        widths,
        keep_mask,
        own,
        halo,
        cot,
        mats["own"],
        mats["halo"],
        mats["cot"],
        mats["out"],
        col,
        bias,
        vecs,
        up_bias.astype(F32)[None, :],
        in_weight,
        out_weight,
        up_weight,
        down_weight,
    )
    grad_own, grad_halo, acc_two, table = pl.pallas_call(
        backward_kernel,
        grid=grid,
        in_specs=[
            in_smem(),
            by_image((padded, channels)),
            by_image((padded, 3 * channels)),
            by_image((pairs, groups, 2 * PAD, GROUP * PAD)),
            by_image((padded, channels)),
            by_image((padded, channels)),
            whole((area - edge, padded)),
            whole((edge, padded)),
            whole((padded, 1)),
            whole((16, channels)),
            whole((channels, 3 * channels)),
        ],
        out_specs=[
            by_image((area - edge, channels)),
            by_image((edge, channels)),
            kept((rows_two, channels)),
            kept((groups, PAD, GROUP * PAD)),
        ],
        out_shape=[
            jax.ShapeDtypeStruct((images, area - edge, channels), F32),
            jax.ShapeDtypeStruct((images, edge, channels), BF16),
            jax.ShapeDtypeStruct((rows_two, channels), F32),
            jax.ShapeDtypeStruct((groups, PAD, GROUP * PAD), F32),
        ],
        scratch_shapes=[pltpu.VMEM((padded, 3 * channels), BF16)],
        compiler_params=params,
        interpret=interpret,
        name="attention_back",
    )(
        widths,
        xs,
        qkv,
        probs,
        grad_after,
        grad_mixed,
        mats["own_t"],
        mats["halo_t"],
        col,
        vecs,
        in_weight,
    )
    received = lax.ppermute(grad_halo, "rows", [(n, (n + 1) % count) for n in range(count)])
    grad_patches = jnp.concatenate([received.astype(F32), grad_own], axis=1).reshape(
        images, height, columns, channels
    )
    pairs_grad = table.reshape(groups, PAD, GROUP, PAD)[:, :TOK, :, :TOK]
    pairs_grad = pairs_grad.transpose(0, 2, 1, 3).reshape(HEADS, TOK * TOK)
    grad_table = lax.dot_general(
        pair_offsets().astype(F32).reshape(-1, TOK * TOK),
        pairs_grad,
        (((1,), (1,)), ((), ())),
        precision=lax.Precision.HIGHEST,
        preferred_element_type=F32,
    )
    table_size = grad_table.size
    table_rows = -(-table_size // channels)
    flat = jnp.pad(grad_table.reshape(-1), (0, table_rows * channels - table_size))
    small_two = 3 * channels
    acc_two = lax.dynamic_update_slice(acc_two, flat.reshape(table_rows, channels), (small_two + 4, 0))

    one = jnp.concatenate(summed_over_devices(acc_one, (1280, 1280, 1024), sizes)).astype(F32)
    two = jnp.concatenate(summed_over_devices(acc_two, (512, 768), sizes)).astype(F32)
    grad_down_w = one[:hidden]
    grad_up_w = jnp.concatenate(
        [one[hidden + c * channels : hidden + (c + 1) * channels] for c in range(chunks)], axis=1
    )
    grad_out_w = one[2 * hidden : 2 * hidden + channels]
    s = 2 * hidden + channels
    grad_in_w = jnp.concatenate(
        [two[c * channels : (c + 1) * channels] for c in range(3)], axis=1
    )
    return (
        output.reshape(images, height, columns, channels),
        grad_patches,
        two[small_two],
        two[small_two + 1],
        grad_in_w,
        jnp.concatenate([two[small_two + 2], two[small_two + 3]]),
        two[small_two + 4 : small_two + 4 + table_rows].reshape(-1)[:table_size].reshape(
            grad_table.shape
        ),
        grad_out_w,
        one[s + 2],
        one[s],
        one[s + 1],
        grad_up_w,
        one[s + 4 : s + 4 + chunks].reshape(-1),
        grad_down_w,
        one[s + 3],
    )


def solution(mesh, interpret=False):
    sizes = dict(mesh.shape)
    canvas = P("batch", "rows", None, None)
    placed = (canvas, P("batch"), P("batch", None)) + (P(),) * 13 + (canvas,)

    def body(*args):
        return on_device(sizes, interpret, *args)

    return jax.shard_map(
        body,
        mesh=mesh,
        in_specs=placed,
        out_specs=(canvas, canvas) + (P(),) * 13,
        check_vma=False,
    )
```

```python
import math

import jax
import jax.numpy as jnp
from jax import lax
from jax.experimental import pallas as pl
from jax.experimental.pallas import tpu as pltpu
from jax.sharding import PartitionSpec as P

HEADS = 12
WIN = 7
SHIFT = 3
TOK = WIN * WIN
PAD = 56
GROUP = 4

EPSILON = 1e-05
KEEP_RATE = 0.8
MASKED = -100.0
EMPTY = -1e30

F32 = jnp.float32
BF16 = jnp.bfloat16


def nn(a, b):
    return lax.dot_general(a, b, (((1,), (0,)), ((), ())), preferred_element_type=F32)


def nt(a, b):
    return lax.dot_general(a, b, (((1,), (1,)), ((), ())), preferred_element_type=F32)


def tn(a, b):
    return lax.dot_general(a, b, (((0,), (0,)), ((), ())), preferred_element_type=F32)


def col_sum(a):
    return jnp.sum(a, axis=0, keepdims=True)


def row_mean(a):
    return jnp.mean(a, axis=-1, keepdims=True)


def normed(v):
    centred = v - row_mean(v)
    root = lax.rsqrt(row_mean(centred * centred) + EPSILON)
    return centred * root, root


def head_masks():
    lane = lax.broadcasted_iota(jnp.int32, (PAD, 128), 1)
    return [(lane >= 32 * h) & (lane < 32 * (h + 1)) for h in range(GROUP)]


def stacked(pair, masks):
    a, b = pair[:PAD], pair[PAD:]
    rows = [
        jnp.concatenate([jnp.where(m, a, 0.0), jnp.where(m, b, 0.0)], axis=1) for m in masks
    ]
    return jnp.concatenate(rows, axis=0).astype(BF16)


def diagonal(pair):
    a, b = pair[:PAD], pair[PAD:]
    z = jnp.zeros_like(a)
    return jnp.concatenate(
        [jnp.concatenate([a, z], axis=1), jnp.concatenate([z, b], axis=1)], axis=0
    ).astype(BF16)


def undiagonal(m):
    return jnp.concatenate([m[:PAD, :128], m[PAD:, 128:]], axis=0)


def unstacked(m, masks):
    sides = []
    for side in range(2):
        total = None
        for h, mask in enumerate(masks):
            piece = jnp.where(mask, m[h * PAD : (h + 1) * PAD, side * 128 : (side + 1) * 128], 0.0)
            total = piece if total is None else total + piece
        sides.append(total)
    return jnp.concatenate(sides, axis=0)


def normal_cdf_pdf(v):
    e = jnp.exp(-0.5 * (v * v))
    t = 1.0 / (1.0 + (0.3275911 / math.sqrt(2.0)) * jnp.abs(v))
    poly = 1.061405429
    for c in (-1.453152027, 1.421413741, -0.284496736, 0.254829592):
        poly = poly * t + c
    half_tail = (0.5 * poly) * t * e
    cdf = jnp.where(v >= 0.0, 1.0 - half_tail, half_tail)
    return cdf, e * (1.0 / math.sqrt(2.0 * math.pi))


def forward_kernel(
    widths_ref,
    keep_ref,
    own_ref,
    halo_ref,
    cot_ref,
    p_own_ref,
    p_halo_ref,
    p_cot_ref,
    p_out_ref,
    col_ref,
    bias_ref,
    vec_ref,
    up_bias_ref,
    in_w_ref,
    out_w_ref,
    up_w_ref,
    down_w_ref,
    out_ref,
    xs_ref,
    qkv_ref,
    prob_ref,
    grad_after_ref,
    grad_mixed_ref,
    acc_ref,
    proj_sc,
    mixed_sc,
    down_sc,
):
    i = pl.program_id(0)
    last = pl.num_programs(0) - 1
    channels = own_ref.shape[-1]
    hidden = up_w_ref.shape[1]
    chunks = hidden // channels
    groups = channels // 128
    pairs = proj_sc.shape[0] // (2 * PAD)
    factor = 1.0 / math.sqrt(channels // HEADS)

    @pl.when(i == 0)
    def _():
        acc_ref[...] = jnp.zeros_like(acc_ref)
        down_sc[...] = jnp.zeros_like(down_sc)

    def vec(n):
        return vec_ref[n : n + 1, :]

    valid = (col_ref[...] < widths_ref[i]).astype(F32)
    ka = keep_ref[i, 0].astype(F32) / KEEP_RATE
    kb = keep_ref[i, 1].astype(F32) / KEEP_RATE
    valid_a = valid * ka
    valid_b = valid * kb

    xs = nn(p_own_ref[...], own_ref[0]) + nn(p_halo_ref[...], halo_ref[0])
    xs_ref[0] = xs.astype(BF16)
    norm_one, _ = normed(xs)
    hidden_one = ((norm_one * vec(0) + vec(1)) * valid).astype(BF16)
    for part in range(3):
        cols = slice(part * channels, (part + 1) * channels)
        projected = nn(hidden_one, in_w_ref[:, cols]) + vec(2 + part)
        proj_sc[:, cols] = projected
        qkv_ref[0, :, cols] = projected.astype(BF16)

    masks = head_masks()

    def one_pair(j, carry):
        rows = pl.ds(pl.multiple_of(j * 2 * PAD, 2 * PAD), 2 * PAD)
        edge = (j == pairs - 1).astype(jnp.int32)
        for g in range(groups):
            lanes = [
                slice(part * channels + g * 128, part * channels + (g + 1) * 128)
                for part in range(3)
            ]
            q = stacked(proj_sc[rows, lanes[0]], masks)
            k = diagonal(proj_sc[rows, lanes[1]])
            v = diagonal(proj_sc[rows, lanes[2]])
            scores = nt(k, q) * factor + bias_ref[edge, g]
            probs = []
            for side in (scores[:PAD], scores[PAD:]):
                e = jnp.exp(side - jnp.max(side, axis=0, keepdims=True))
                probs.append(e * (1.0 / col_sum(e)))
            probs = jnp.concatenate(probs, axis=0).astype(BF16)
            prob_ref[0, j, g] = probs
            mixed_sc[rows, lanes[0]] = unstacked(tn(probs, v), masks)
        return carry

    lax.fori_loop(0, pairs, one_pair, 0)

    mixed = mixed_sc[...].astype(BF16)
    after = xs + valid_a * (nn(mixed, out_w_ref[...]) + vec(5))
    norm_two, root_two = normed(after)
    hidden_two = (norm_two * vec(6) + vec(7)).astype(BF16)
    cot = nn(p_cot_ref[...], cot_ref[0])
    grad_mlp_wide = (cot * valid_b).astype(BF16)
    mlp = jnp.zeros_like(after)
    grad_hidden = jnp.zeros_like(after)
    up_base = hidden
    small = 2 * hidden + channels
    for c in range(chunks):
        cols = slice(c * channels, (c + 1) * channels)
        pre = nn(hidden_two, up_w_ref[:, cols]) + up_bias_ref[:, cols]
        cdf, pdf = normal_cdf_pdf(pre)
        act = (pre * cdf).astype(BF16)
        mlp = mlp + nn(act, down_w_ref[cols, :])
        grad_act = nt(grad_mlp_wide, down_w_ref[cols, :])
        grad_pre = (grad_act * (cdf + pre * pdf)).astype(BF16)
        grad_hidden = grad_hidden + nt(grad_pre, up_w_ref[:, cols])
        up_rows = slice(up_base + c * channels, up_base + (c + 1) * channels)
        acc_ref[up_rows, :] += tn(hidden_two, grad_pre)
        down_sc[:, cols] += tn(grad_mlp_wide, act)
        acc_ref[small + 4 + c : small + 5 + c, :] += col_sum(grad_pre.astype(F32))
    result = (after + valid_b * (mlp + vec(8))).astype(BF16)
    out_ref[0] = nn(p_out_ref[...], result).astype(BF16)

    d = grad_hidden * vec(6)
    grad_after = cot + root_two * (d - row_mean(d) - norm_two * row_mean(d * norm_two))
    grad_after_ref[0] = grad_after
    grad_attn = (grad_after * valid_a).astype(BF16)
    grad_mixed_ref[0] = nt(grad_attn, out_w_ref[...]).astype(BF16)
    acc_ref[2 * hidden : 2 * hidden + channels, :] += tn(mixed, grad_attn)
    acc_ref[small : small + 1, :] += col_sum(grad_hidden * norm_two)
    acc_ref[small + 1 : small + 2, :] += col_sum(grad_hidden)
    acc_ref[small + 2 : small + 3, :] += col_sum(grad_attn.astype(F32))
    acc_ref[small + 3 : small + 4, :] += col_sum(grad_mlp_wide.astype(F32))

    @pl.when(i == last)
    def _():
        for c in range(chunks):
            cols = slice(c * channels, (c + 1) * channels)
            acc_ref[cols, :] = down_sc[:, cols].T


def backward_kernel(
    widths_ref,
    xs_ref,
    qkv_ref,
    prob_ref,
    grad_after_ref,
    grad_mixed_ref,
    p_own_t_ref,
    p_halo_t_ref,
    col_ref,
    vec_ref,
    in_w_ref,
    grad_own_ref,
    grad_halo_ref,
    acc_ref,
    proj_sc,
):
    i = pl.program_id(0)
    channels = xs_ref.shape[-1]
    groups = channels // 128
    pairs = proj_sc.shape[0] // (2 * PAD)
    factor = 1.0 / math.sqrt(channels // HEADS)

    @pl.when(i == 0)
    def _():
        acc_ref[...] = jnp.zeros_like(acc_ref)

    def vec(n):
        return vec_ref[n : n + 1, :]

    valid = (col_ref[...] < widths_ref[i]).astype(F32)
    masks = head_masks()

    def one_pair(j, carry):
        rows = pl.ds(pl.multiple_of(j * 2 * PAD, 2 * PAD), 2 * PAD)
        for g in range(groups):
            lanes = [
                slice(part * channels + g * 128, part * channels + (g + 1) * 128)
                for part in range(3)
            ]
            pair_q = qkv_ref[0, rows, lanes[0]].astype(F32)
            pair_k = qkv_ref[0, rows, lanes[1]].astype(F32)
            pair_v = qkv_ref[0, rows, lanes[2]].astype(F32)
            pair_m = grad_mixed_ref[0, rows, lanes[0]].astype(F32)
            q = stacked(pair_q, masks)
            gm = stacked(pair_m, masks)
            k = diagonal(pair_k)
            v = diagonal(pair_v)
            probs_low = prob_ref[0, j, g]
            probs = probs_low.astype(F32)
            grad_v = undiagonal(nn(probs_low, gm))
            weighted = probs * nt(v, gm)
            scores = []
            for lo in (0, PAD):
                side = weighted[lo : lo + PAD]
                scores.append(side - probs[lo : lo + PAD] * col_sum(side))
            first = 3 * channels + 8 + g * PAD
            acc_ref[first : first + PAD, : GROUP * PAD] += scores[0] + scores[1]
            grad_s = jnp.concatenate(scores, axis=0).astype(BF16)
            grad_k = undiagonal(nn(grad_s, q)) * factor
            grad_q = unstacked(tn(grad_s, k), masks) * factor
            proj_sc[rows, lanes[0]] = grad_q.astype(BF16)
            proj_sc[rows, lanes[1]] = grad_k.astype(BF16)
            proj_sc[rows, lanes[2]] = grad_v.astype(BF16)
        return carry

    lax.fori_loop(0, pairs, one_pair, 0)

    norm_one, root_one = normed(xs_ref[0].astype(F32))
    hidden_one = ((norm_one * vec(0) + vec(1)) * valid).astype(BF16)
    grad_hidden = jnp.zeros_like(norm_one)
    small = 3 * channels
    for part in range(3):
        cols = slice(part * channels, (part + 1) * channels)
        grad_proj = proj_sc[:, cols]
        acc_ref[cols, :] += tn(hidden_one, grad_proj)
        grad_hidden = grad_hidden + nt(grad_proj, in_w_ref[:, cols])
        if part != 1:
            row = small + 2 + part // 2
            acc_ref[row : row + 1, :] += col_sum(grad_proj.astype(F32))
    grad_hidden = grad_hidden * valid
    acc_ref[small : small + 1, :] += col_sum(grad_hidden * norm_one)
    acc_ref[small + 1 : small + 2, :] += col_sum(grad_hidden)
    d = grad_hidden * vec(0)
    grad_xs = grad_after_ref[0] + root_one * (
        d - row_mean(d) - norm_one * row_mean(d * norm_one)
    )
    high = grad_xs.astype(BF16)
    rest = (grad_xs - high.astype(F32)).astype(BF16)
    p_own_t = p_own_t_ref[...]
    grad_own_ref[0] = nn(p_own_t, high) + nn(p_own_t, rest)
    grad_halo_ref[0] = nn(p_halo_t_ref[...], high).astype(BF16)


def placements(height, columns):
    row = jnp.arange(columns // WIN * PAD, dtype=jnp.int32)
    place = row % PAD
    real = place < TOK
    s = jnp.where(real, place // WIN, 1000)
    t = row // PAD * WIN + place % WIN
    shifted = (t + SHIFT) % columns
    own = jnp.where(s < height - SHIFT, (s + SHIFT) * columns + shifted, -1)
    halo = jnp.where((s >= height - SHIFT) & real, (s - height + SHIFT) * columns + shifted, -1)
    plain = jnp.where(real, s * columns + t, -1)

    def hot(index, count, first=0):
        return index[:, None] == first + jnp.arange(count, dtype=jnp.int32)[None, :]

    def hot_t(index, count, first=0):
        return index[None, :] == first + jnp.arange(count, dtype=jnp.int32)[:, None]

    area = height * columns
    edge = SHIFT * columns
    mats = dict(
        own=hot(own, area),
        halo=hot(halo, edge),
        cot=hot(plain, area),
        out=hot_t(plain, area),
        own_t=hot_t(own, area - edge, edge),
        halo_t=hot_t(halo, edge),
    )
    col = jnp.where(real, shifted, 1 << 20)
    return {k: v.astype(BF16) for k, v in mats.items()}, col[:, None]


def pair_offsets():
    a = jnp.arange(TOK, dtype=jnp.int32)
    r, c = a // WIN, a % WIN
    span = 2 * WIN - 1
    index = (r[None, :] - r[:, None] + WIN - 1) * span + c[None, :] - c[:, None] + WIN - 1
    return index[None] == jnp.arange(span * span, dtype=jnp.int32)[:, None, None]


def score_bias(bias_table, last_row):
    hot = pair_offsets().astype(BF16).reshape(-1, TOK * TOK)
    bias = lax.dot_general(
        bias_table, hot, (((0,), (0,)), ((), ())), preferred_element_type=F32
    ).reshape(HEADS, TOK, TOK)
    a = jnp.arange(TOK, dtype=jnp.int32)
    cut = WIN - SHIFT
    row_region = (a // WIN >= cut) & last_row
    col_region = a % WIN >= cut
    row_same = row_region[:, None] == row_region[None, :]
    col_same = col_region[:, None] == col_region[None, :]
    inner = jnp.where(row_same, 0.0, MASKED).astype(F32)
    edge = jnp.where(row_same & col_same, 0.0, MASKED).astype(F32)

    def laid(mask):
        full = jnp.pad(
            bias + mask[None], ((0, 0), (0, 0), (0, PAD - TOK)), constant_values=0.0
        )
        full = jnp.pad(full, ((0, 0), (0, PAD - TOK), (0, 0)), constant_values=EMPTY)
        full = full.reshape(HEADS // GROUP, GROUP, PAD, PAD).transpose(0, 2, 1, 3)
        return full.reshape(HEADS // GROUP, PAD, GROUP * PAD)

    plain, right = laid(inner), laid(edge)
    return jnp.stack(
        [jnp.concatenate([plain, plain], axis=1), jnp.concatenate([plain, right], axis=1)]
    )


def whole(shape):
    return pl.BlockSpec(shape, lambda i: (0,) * len(shape), pipeline_mode=pl.Buffered(1))


def kept(shape):
    return pl.BlockSpec(shape, lambda i: (0,) * len(shape))


def by_image(shape):
    return pl.BlockSpec((1,) + shape, lambda i: (i,) + (0,) * len(shape))


def in_smem():
    return pl.BlockSpec(memory_space=pltpu.SMEM)


def power_bits(count):
    bits = count.bit_length() - 1
    assert 1 << bits == count
    return bits


def chip_orders(sizes):
    low = power_bits(sizes["batch"])
    rows = [low + b for b in range(power_bits(sizes["rows"]))]
    batch = list(range(1, low))
    lead = batch[:1] + rows[:2]
    rest = rows[2:] + batch[1:]
    return [lead + rest, lead[-1:] + lead[:-1] + rest]


def swapped(value, bits):
    total = lax.axis_size("rows") * lax.axis_size("batch")
    pairs = [(n, n ^ (1 << bits[n & 1])) for n in range(total)]
    return lax.ppermute(value, ("rows", "batch"), pairs)


def my_bit(bits):
    index = lax.axis_index("rows") * lax.axis_size("batch") + lax.axis_index("batch")
    return jnp.where(index & 1 == 0, index >> bits[0], index >> bits[1]) & 1


def halves(value, bit):
    half = value.shape[0] // 2
    return (
        lax.dynamic_slice_in_dim(value, bit * half, half),
        lax.dynamic_slice_in_dim(value, (1 - bit) * half, half),
    )


def ordered(bit, mine, other):
    return jnp.where(
        bit == 0, jnp.concatenate([mine, other]), jnp.concatenate([other, mine])
    )


def summed_over_devices(values, sizes):
    core = (0, 0)
    steps = list(zip(*chip_orders(sizes)))
    bit = my_bit(core)
    split = [halves(v, bit) for v in values]
    sent = jnp.concatenate([away.astype(BF16) for _, away in split])
    kept_rows = jnp.concatenate([keep for keep, _ in split])
    part = kept_rows + swapped(sent, core).astype(F32)
    for bits in steps:
        keep, away = halves(part, my_bit(bits))
        part = keep + swapped(away.astype(BF16), bits).astype(F32)
    part = part.astype(BF16)
    for bits in reversed(steps):
        part = ordered(my_bit(bits), part, swapped(part, bits))
    other = swapped(part, core)
    sums, start = [], 0
    for v in values:
        rows = slice(start, start + v.shape[0] // 2)
        sums.append(ordered(bit, part[rows], other[rows]))
        start = rows.stop
    return sums


def on_device(sizes, interpret, *args):
    (
        patches,
        widths,
        keep_mask,
        pre_gain,
        pre_shift,
        in_weight,
        in_bias,
        bias_table,
        out_weight,
        out_bias,
        mid_gain,
        mid_shift,
        up_weight,
        up_bias,
        down_weight,
        down_bias,
        cotangent,
    ) = args
    images, height, columns, channels = patches.shape
    hidden = up_weight.shape[1]
    area = height * columns
    edge = SHIFT * columns
    count = lax.axis_size("rows")
    padded = columns // WIN * PAD
    pairs = columns // WIN // 2
    groups = channels // 128
    chunks = hidden // channels

    halo = lax.ppermute(
        patches[:, :SHIFT].reshape(images, edge, channels),
        "rows",
        [(n, (n - 1) % count) for n in range(count)],
    )
    own = patches.reshape(images, area, channels)
    cot = cotangent.reshape(images, area, channels)
    mats, col = placements(height, columns)
    bias = score_bias(bias_table, lax.axis_index("rows") == count - 1)
    zero = jnp.zeros((channels,), F32)
    vecs = jnp.stack(
        [
            pre_gain.astype(F32),
            pre_shift.astype(F32),
            in_bias[:channels].astype(F32),
            zero,
            in_bias[channels:].astype(F32),
            out_bias.astype(F32),
            mid_gain.astype(F32),
            mid_shift.astype(F32),
            down_bias.astype(F32),
        ]
        + [zero] * 7
    )
    grid = (images,)
    params = pltpu.CompilerParams(
        dimension_semantics=("arbitrary",), vmem_limit_bytes=60 * 1024 * 1024
    )
    rows_one = 2 * hidden + channels + 64
    rows_two = 3 * channels + 192
    output, xs, qkv, probs, grad_after, grad_mixed, acc_one = pl.pallas_call(
        forward_kernel,
        grid=grid,
        in_specs=[
            in_smem(),
            in_smem(),
            by_image((area, channels)),
            by_image((edge, channels)),
            by_image((area, channels)),
            whole((padded, area)),
            whole((padded, edge)),
            whole((padded, area)),
            whole((area, padded)),
            whole((padded, 1)),
            whole(bias.shape),
            whole((16, channels)),
            whole((1, hidden)),
            whole((channels, 3 * channels)),
            whole((channels, channels)),
            whole((channels, hidden)),
            whole((hidden, channels)),
        ],
        out_specs=[
            by_image((area, channels)),
            by_image((padded, channels)),
            by_image((padded, 3 * channels)),
            by_image((pairs, groups, 2 * PAD, GROUP * PAD)),
            by_image((padded, channels)),
            by_image((padded, channels)),
            kept((rows_one, channels)),
        ],
        out_shape=[
            jax.ShapeDtypeStruct((images, area, channels), BF16),
            jax.ShapeDtypeStruct((images, padded, channels), BF16),
            jax.ShapeDtypeStruct((images, padded, 3 * channels), BF16),
            jax.ShapeDtypeStruct((images, pairs, groups, 2 * PAD, GROUP * PAD), BF16),
            jax.ShapeDtypeStruct((images, padded, channels), F32),
            jax.ShapeDtypeStruct((images, padded, channels), BF16),
            jax.ShapeDtypeStruct((rows_one, channels), F32),
        ],
        scratch_shapes=[
            pltpu.VMEM((padded, 3 * channels), F32),
            pltpu.VMEM((padded, channels), F32),
            pltpu.VMEM((channels, hidden), F32),
        ],
        compiler_params=params,
        interpret=interpret,
        name="forward_mlp",
    )(
        widths,
        keep_mask,
        own,
        halo,
        cot,
        mats["own"],
        mats["halo"],
        mats["cot"],
        mats["out"],
        col,
        bias,
        vecs,
        up_bias.astype(F32)[None, :],
        in_weight,
        out_weight,
        up_weight,
        down_weight,
    )
    grad_own, grad_halo, acc_two = pl.pallas_call(
        backward_kernel,
        grid=grid,
        in_specs=[
            in_smem(),
            by_image((padded, channels)),
            by_image((padded, 3 * channels)),
            by_image((pairs, groups, 2 * PAD, GROUP * PAD)),
            by_image((padded, channels)),
            by_image((padded, channels)),
            whole((area - edge, padded)),
            whole((edge, padded)),
            whole((padded, 1)),
            whole((16, channels)),
            whole((channels, 3 * channels)),
        ],
        out_specs=[
            by_image((area - edge, channels)),
            by_image((edge, channels)),
            kept((rows_two, channels)),
        ],
        out_shape=[
            jax.ShapeDtypeStruct((images, area - edge, channels), F32),
            jax.ShapeDtypeStruct((images, edge, channels), BF16),
            jax.ShapeDtypeStruct((rows_two, channels), F32),
        ],
        scratch_shapes=[pltpu.VMEM((padded, 3 * channels), BF16)],
        compiler_params=params,
        interpret=interpret,
        name="attention_back",
    )(
        widths,
        xs,
        qkv,
        probs,
        grad_after,
        grad_mixed,
        mats["own_t"],
        mats["halo_t"],
        col,
        vecs,
        in_weight,
    )
    received = lax.ppermute(grad_halo, "rows", [(n, (n + 1) % count) for n in range(count)])
    grad_patches = jnp.concatenate([received.astype(F32), grad_own], axis=1).reshape(
        images, height, columns, channels
    )
    small_two = 3 * channels
    one, two = summed_over_devices((acc_one, acc_two), sizes)
    table = two[small_two + 8 : small_two + 8 + groups * PAD, : GROUP * PAD]
    table = table.reshape(groups, PAD, GROUP, PAD)[:, :TOK, :, :TOK]
    table = table.transpose(0, 2, 1, 3).reshape(HEADS, TOK * TOK)
    grad_table = lax.dot_general(
        pair_offsets().astype(BF16).reshape(-1, TOK * TOK),
        table,
        (((1,), (1,)), ((), ())),
        preferred_element_type=F32,
    )
    one = one.astype(F32)
    two = two.astype(F32)
    grad_down_w = one[:hidden]
    grad_up_w = jnp.concatenate(
        [one[hidden + c * channels : hidden + (c + 1) * channels] for c in range(chunks)], axis=1
    )
    grad_out_w = one[2 * hidden : 2 * hidden + channels]
    s = 2 * hidden + channels
    grad_in_w = jnp.concatenate(
        [two[c * channels : (c + 1) * channels] for c in range(3)], axis=1
    )
    return (
        output.reshape(images, height, columns, channels),
        grad_patches,
        two[small_two],
        two[small_two + 1],
        grad_in_w,
        jnp.concatenate([two[small_two + 2], two[small_two + 3]]),
        grad_table,
        grad_out_w,
        one[s + 2],
        one[s],
        one[s + 1],
        grad_up_w,
        one[s + 4 : s + 4 + chunks].reshape(-1),
        grad_down_w,
        one[s + 3],
    )


def solution(mesh, interpret=False):
    sizes = dict(mesh.shape)
    canvas = P("batch", "rows", None, None)
    placed = (canvas, P("batch"), P("batch", None)) + (P(),) * 13 + (canvas,)

    def body(*args):
        return on_device(sizes, interpret, *args)

    return jax.shard_map(
        body,
        mesh=mesh,
        in_specs=placed,
        out_specs=(canvas, canvas) + (P(),) * 13,
        check_vma=False,
    )
```
